32 devices in a mesh: slab: 4 (over x, core), pos: 8 (over z, y).
Axes of the slice: x: 2, y: 2, z: 4, core: 2. Of those that a mesh axis runs over, the one named last changes fastest.
Arguments:
- object_field: float32 [2, 4, 1024, 2048], P(None, 'slab', 'pos'), may hold values from -0.25 to 1.15, as said below
- probe_wave: float32 [2, 128, 128], replicated, may hold values from -4.2 to 4.2
- scan_coords: int32 [24, 2], P('pos'), may hold values from 0 to 1920, as said below
- scan_counts: int32 [8], P('pos'), may hold values from 1 to 3, as said below
- measured: float32 [24, 128, 128], P('pos'), may hold values from 0.1 to 3
Outputs:
- object_gradient: float32 [2, 4, 1024, 2048], P(None, 'slab', 'pos')
The draws below stay inside these ranges and needn't reach their ends.
Inputs may be any that keep to these rules, and one draw needn't show every extreme that they name: `object_field`: real parts between 0.85 and 1.15, imaginary parts between -0.25 and 0.25. `scan_coords`: slot q belongs to owner j = q div 3; its row corner lies in [j * 128, (j + 1) * 128) and is at most 896; its column corner is at most 1920. The first scan_counts[j] slots of owner j are live, the others are not; some owner has all 3 live.
All inputs are finite; a program needn't handle non-finite values.
Results may differ from the reference program's by a relative error of at most 0.02.
Values may be sent and summed in bfloat16 or wider, within the bound.
No kernel may reach another device: no remote copies, remote signals or barrier semaphores. Data moves between devices by JAX's collectives and lax.ppermute only.
A program may use at most 64 MiB of HBM per device.

```python
import math
import jax
import jax.numpy as jnp
from jax import lax

P_SIZE = 128
NCOL = 2048
ROWS_DEV = 128
SL_DEV = 1
CAP = 3
SLICES = 4
NOBJ = 1024
SLOTS = 24
N_POS = 8


def draw_object_field(key, part):
    real_part = jax.random.uniform(jax.random.fold_in(key, 31), (SLICES, NOBJ, NCOL), jnp.float32, 0.85, 1.15)
    imag_part = jax.random.uniform(jax.random.fold_in(key, 32), (SLICES, NOBJ, NCOL), jnp.float32, -0.25, 0.25)
    return jnp.stack([real_part, imag_part]).astype(jnp.float32)


def draw_scan_coords(key, part):
    slot_ids = jnp.arange(SLOTS, dtype=jnp.int32)
    owner_ids = slot_ids // CAP
    offsets = jax.random.randint(jax.random.fold_in(key, 11), (SLOTS,), 0, ROWS_DEV, dtype=jnp.int32)
    corner_rows = jnp.minimum(owner_ids * ROWS_DEV + offsets, NOBJ - P_SIZE)
    corner_cols = jax.random.randint(jax.random.fold_in(key, 12), (SLOTS,), 0, NCOL - P_SIZE + 1, dtype=jnp.int32)
    corner_rows = jnp.where(slot_ids == 0, 0, corner_rows)
    corner_cols = jnp.where(slot_ids == 0, 0, corner_cols)
    corner_cols = jnp.where(slot_ids == 1, NCOL - P_SIZE, corner_cols)
    return jnp.stack([corner_rows, corner_cols], axis=1).astype(jnp.int32)


def draw_scan_counts(key, part):
    base_counts = jax.random.randint(jax.random.fold_in(key, 21), (N_POS,), 1, CAP + 1, dtype=jnp.int32)
    chosen = jax.random.randint(jax.random.fold_in(key, 22), (), 0, N_POS, dtype=jnp.int32)
    owner_ids = jnp.arange(N_POS, dtype=jnp.int32)
    return jnp.where(owner_ids == chosen, CAP, base_counts).astype(jnp.int32)


def level_of(own_key, dims, shards, smallest, high):
    factor_of = 1.0
    for axis_at, parts in shards:
        steps = jax.random.uniform(jax.random.fold_in(jax.random.fold_in(own_key, 6), axis_at), (parts,), jnp.float32, smallest / len(shards), high / len(shards))
        factor_of = factor_of * jnp.repeat(jnp.exp(steps), dims[axis_at] // parts).reshape((-1,) + (1,) * (len(dims) - 1 - axis_at))
    return factor_of


def normal_values(rng, dims, deviation, most, kind=jnp.bfloat16):
    entries = jax.random.normal(rng, dims, jnp.float32) * deviation
    return jnp.minimum(jnp.maximum(entries, -most), most).astype(kind)


def setup_inputs(seed: int = 0) -> dict:
    key_list = jax.random.split(jax.random.key(seed), 6)
    return {
        "object_field": draw_object_field(jax.random.fold_in(key_list[5], 71), 0),
        "probe_wave": normal_values(key_list[1], (2, P_SIZE, P_SIZE), 0.7, 4.2, jnp.float32),
        "scan_coords": draw_scan_coords(jax.random.fold_in(key_list[5], 71), 0),
        "scan_counts": draw_scan_counts(jax.random.fold_in(key_list[5], 71), 0),
        "measured": jnp.clip(jnp.exp(math.log(3.0) - 3.4011974 * jax.random.uniform(key_list[4], (SLOTS, P_SIZE, P_SIZE), jnp.float32) ** level_of(key_list[4], (SLOTS, P_SIZE, P_SIZE), ((0, 8),), -0.2, 0.2)), 0.1, 3.0),
    }


spread_factor = 0.5

def fourier_tables(length):
    grid_index = jnp.arange(length, dtype=jnp.int32)
    phase_index = grid_index[:, None] * grid_index[None, :] % length
    angles = phase_index.astype(jnp.float32) * (2.0 * math.pi / length)
    norm_factor = 1.0 / math.sqrt(length)
    return (jnp.cos(angles) * norm_factor, -jnp.sin(angles) * norm_factor)

def kernel_table(length):
    grid_index = jnp.arange(length, dtype=jnp.int32)
    centred = (grid_index + length // 2) % length - length // 2
    squares = centred[:, None] * centred[:, None] + centred[None, :] * centred[None, :]
    phases = squares.astype(jnp.float32) * (spread_factor / length)
    return jnp.stack([jnp.cos(phases), -jnp.sin(phases)])

def left_apply(real_table, imag_table, field):

    def multiply(matrix, field_block):
        return jnp.einsum('ij,bjk->bik', matrix, field_block, precision=lax.Precision.HIGHEST)
    return jnp.stack([multiply(real_table, field[0]) - multiply(imag_table, field[1]), multiply(real_table, field[1]) + multiply(imag_table, field[0])])

def right_apply(field, real_table, imag_table):

    def multiply(field_block, matrix):
        return jnp.einsum('bij,jk->bik', field_block, matrix, precision=lax.Precision.HIGHEST)
    return jnp.stack([multiply(field[0], real_table) - multiply(field[1], imag_table), multiply(field[1], real_table) + multiply(field[0], imag_table)])

def transform(field, real_table, imag_table):
    return right_apply(left_apply(real_table, imag_table, field), real_table, imag_table)

def product(left_op, right_op):
    return jnp.stack([left_op[0] * right_op[0] - left_op[1] * right_op[1], left_op[0] * right_op[1] + left_op[1] * right_op[0]])

def conj_product(left_op, right_op):
    return jnp.stack([left_op[0] * right_op[0] + left_op[1] * right_op[1], left_op[0] * right_op[1] - left_op[1] * right_op[0]])

def propagate(field, real_table, imag_table, kernel):
    spectrum = transform(field, real_table, imag_table)
    return transform(product(kernel[:, None], spectrum), real_table, -imag_table)

def back_propagate(field, real_table, imag_table, kernel):
    spectrum = transform(field, real_table, imag_table)
    return transform(conj_product(kernel[:, None], spectrum), real_table, -imag_table)

def detector(wave_field, measured, live_mask, real_table, imag_table):
    far_field = transform(wave_field, real_table, imag_table)
    intensity = far_field[0] * far_field[0] + far_field[1] * far_field[1]
    weight = (intensity - measured) * live_mask[:, None, None]
    return transform(far_field * weight[None], real_table, -imag_table)

def rounded(field):
    return lax.optimization_barrier(field.astype(jnp.bfloat16)).astype(jnp.float32)

def reference(object_field, probe_wave, scan_coords, scan_counts, measured):
    real_table, imag_table = fourier_tables(P_SIZE)
    kernel = kernel_table(P_SIZE)
    slot_ids = jnp.arange(SLOTS, dtype=jnp.int32)
    owner_ids = slot_ids // CAP
    live_mask = (slot_ids % CAP < scan_counts[owner_ids]).astype(jnp.float32)
    zero_index = jnp.zeros((), jnp.int32)

    def one_slot(gradient, inputs):
        corner_row, corner_col, sample, weight = inputs
        corner_row = corner_row.astype(jnp.int32)
        corner_col = corner_col.astype(jnp.int32)
        offsets = (zero_index, zero_index, corner_row, corner_col)
        patches = lax.dynamic_slice(object_field, offsets, (2, SLICES, P_SIZE, P_SIZE))
        current_wave = probe_wave[:, None]
        kept_waves = []
        for layer_id in range(SLICES):
            if layer_id % SL_DEV == 0 and layer_id > 0:
                current_wave = rounded(current_wave)
            kept_waves.append(current_wave)
            current_wave = propagate(product(current_wave, patches[:, layer_id][:, None]), real_table, imag_table, kernel)
        adjoint = detector(current_wave, sample[None], weight[None], real_table, imag_table)
        pieces = [None] * SLICES
        for layer_id in reversed(range(SLICES)):
            moved = back_propagate(adjoint, real_table, imag_table, kernel)
            pieces[layer_id] = conj_product(kept_waves[layer_id], moved)[:, 0]
            adjoint = conj_product(patches[:, layer_id][:, None], moved)
            if layer_id % SL_DEV == 0 and layer_id > 0:
                adjoint = rounded(adjoint)
        stacked = jnp.stack(pieces, axis=1)
        current = lax.dynamic_slice(gradient, offsets, (2, SLICES, P_SIZE, P_SIZE))
        return (lax.dynamic_update_slice(gradient, current + stacked, offsets), None)
    gradient, unused = lax.scan(one_slot, jnp.zeros(object_field.shape, jnp.float32), (scan_coords[:, 0], scan_coords[:, 1], measured, live_mask))
    return gradient
```

```python
import functools

import jax
import jax.numpy as jnp
import numpy as np
from jax import lax
from jax.experimental import pallas as pl
from jax.experimental.pallas import tpu as pltpu
from jax.sharding import PartitionSpec as P

spread_factor = 0.5

VMEM = pltpu.MemorySpace.VMEM
SMEM = pltpu.MemorySpace.SMEM
ANY = pl.ANY


def chain_tables(length):
    index = np.arange(length)
    phase = (index[:, None] * index[None, :]) % length
    fourier = np.exp(-2j * np.pi * phase / length) / np.sqrt(length)
    centred = (index + length // 2) % length - length // 2
    kernel = np.exp(-1j * spread_factor * centred * centred / length)
    step = np.conj(fourier) @ (kernel[:, None] * fourier)
    tables = []
    for matrix in (step, fourier):
        left = np.block([[matrix.real, -matrix.imag], [matrix.imag, matrix.real]])
        right = np.block([[matrix.real, matrix.imag], [-matrix.imag, matrix.real]])
        for form in (left, right):
            high = form.astype(jnp.bfloat16)
            low = (form - high.astype(np.float64)).astype(jnp.bfloat16)
            tables.append(np.stack([high, low]))
    return np.stack(tables)


def corner(ints, slot, length, blocks):
    row = lax.rem(ints[2 * slot], length)
    col = ints[2 * slot + 1]
    block = jnp.minimum(lax.div(col, length), blocks - 2)
    return row, block, col - block * length


def iota(length, axis):
    return lax.broadcasted_iota(jnp.int32, (length, length), axis)


def strip_copies(ints, strip, window, sems, slots, length, blocks):
    copies = []
    for slot in range(slots):
        _, block, _ = corner(ints, slot, length, blocks)
        start = pl.multiple_of(block * length, length)
        copies.append(
            pltpu.make_async_copy(
                strip.at[:, :, :, pl.ds(start, 2 * length)], window.at[slot], sems.at[slot]
            )
        )
    for copy in copies:
        copy.start()
    return copies


def cut_kernel(ints, strip, tiles, window, sems, *, slots, layers, length, blocks):
    copies = strip_copies(ints, strip, window, sems, slots, length, blocks)
    lanes = iota(length, 1)
    for slot in range(slots):
        _, _, col = corner(ints, slot, length, blocks)
        copies[slot].wait()
        for part in range(2):
            for layer in range(layers):
                block = window[slot, part, layer]
                cut = jnp.where(lanes >= col, block[:, :length], block[:, length:])
                tiles[layer, slot, part] = cut.astype(tiles.dtype)


def merge_kernel(ints, strip, received, tiles, window, sems, *, slots, layers, length, blocks):
    copies = strip_copies(ints, strip, window, sems, slots, length, blocks)
    lanes = iota(length, 1)
    rows = iota(length, 0)
    for slot in range(slots):
        row, _, col = corner(ints, slot, length, blocks)
        copies[slot].wait()
        for part in range(2):
            for layer in range(layers):
                block = window[slot, part, layer]
                cut = jnp.where(lanes >= col, block[:, :length], block[:, length:])
                above = received[layer, slot, part].astype(jnp.float32)
                tiles[layer, slot, part] = jnp.where(rows >= row, above, cut).astype(tiles.dtype)


def chain_kernel(ints, section, *refs, slots, layers, sections, length, blocks):
    gathered = refs[:sections]
    probe, measured, tables, grads, tiles, waves, moved = refs[sections:]
    here = section[0]
    for offset in range(sections):
        start = jnp.bitwise_xor(here, offset) * layers
        for layer in range(layers):
            tiles[start + layer] = gathered[offset][layer]

    def both_sides(real, imag, which):
        field = jnp.concatenate(
            [jnp.concatenate(real, axis=1), jnp.concatenate(imag, axis=1)], axis=0
        ).astype(jnp.bfloat16)
        left = functools.partial(jnp.dot, preferred_element_type=jnp.float32)
        mixed = left(tables[2 * which, 0], field) + left(tables[2 * which, 1], field)
        field = jnp.concatenate(
            [
                jnp.concatenate(
                    [
                        mixed[:length, slot * length : (slot + 1) * length],
                        mixed[length:, slot * length : (slot + 1) * length],
                    ],
                    axis=1,
                )
                for slot in range(slots)
            ],
            axis=0,
        ).astype(jnp.bfloat16)
        mixed = left(field, tables[2 * which + 1, 0]) + left(field, tables[2 * which + 1, 1])
        span = [slice(slot * length, (slot + 1) * length) for slot in range(slots)]
        return [mixed[rows, :length] for rows in span], [mixed[rows, length:] for rows in span]

    def multiply_tile(real, imag, index):
        out_real, out_imag = [], []
        for slot in range(slots):
            tile_real = tiles[index, slot, 0].astype(jnp.float32)
            tile_imag = tiles[index, slot, 1].astype(jnp.float32)
            out_real.append(real[slot] * tile_real - imag[slot] * tile_imag)
            out_imag.append(real[slot] * tile_imag + imag[slot] * tile_real)
        return out_real, out_imag

    def keep(store, index, real, imag):
        for slot in range(slots):
            store[index, slot, 0] = real[slot]
            store[index, slot, 1] = imag[slot]

    real, imag = [], []
    for slot in range(slots):
        row, _, col = corner(ints, slot, length, blocks)
        col = lax.rem(col, length)
        real.append(pltpu.roll(pltpu.roll(probe[0], row, 0), col, 1))
        imag.append(pltpu.roll(pltpu.roll(probe[1], row, 0), col, 1))
    depth = sections * layers
    for index in range(depth):
        keep(waves, index, real, imag)
        real, imag = multiply_tile(real, imag, index)
        real, imag = both_sides(real, imag, 0 if index < depth - 1 else 1)
    live = ints[2 * slots]
    for slot in range(slots):
        intensity = real[slot] * real[slot] + imag[slot] * imag[slot]
        weight = intensity - measured[slot].astype(jnp.float32)
        weight = jnp.where(live > slot, weight, jnp.zeros_like(weight))
        real[slot], imag[slot] = weight * real[slot], -weight * imag[slot]
    for index in reversed(range(depth)):
        real, imag = both_sides(real, imag, 0 if index < depth - 1 else 1)
        keep(moved, index, real, imag)
        if index > 0:
            real, imag = multiply_tile(real, imag, index)
    for layer in range(layers):
        index = here * layers + layer
        for slot in range(slots):
            wave_real, wave_imag = waves[index, slot, 0], waves[index, slot, 1]
            back_real, back_imag = moved[index, slot, 0], moved[index, slot, 1]
            grads[layer, slot, 0] = (wave_real * back_real - wave_imag * back_imag).astype(
                grads.dtype
            )
            grads[layer, slot, 1] = (-wave_real * back_imag - wave_imag * back_real).astype(
                grads.dtype
            )


def add_kernel(own, theirs, lower, upper, out, total, sem, *, slots, layers, length, blocks):
    total[...] = jnp.zeros_like(total)
    lanes = iota(length, 1)
    rows = iota(length, 0)
    for ints, grads, below in ((theirs, lower, True), (own, upper, False)):
        for slot in range(slots):
            row, block, col = corner(ints, slot, length, blocks)
            inside = rows < row if below else rows >= row
            for half in range(2):
                side = lanes >= col if half == 0 else lanes < col
                mask = jnp.logical_and(inside, side)
                span = pl.ds(pl.multiple_of((block + half) * length, length), length)
                for part in range(2):
                    for layer in range(layers):
                        piece = grads[layer, slot, part].astype(jnp.float32)
                        total[part, layer, :, span] += jnp.where(mask, piece, 0.0)
    copy = pltpu.make_async_copy(total, out, sem)
    copy.start()
    copy.wait()


def spec(space):
    return pl.BlockSpec(memory_space=space)


def per_device(object_field, probe_wave, scan_coords, scan_counts, measured):
    length = probe_wave.shape[-1]
    layers = object_field.shape[1]
    assert object_field.shape[2] == length and object_field.shape[3] % length == 0
    blocks = object_field.shape[3] // length
    slots = scan_coords.shape[0]
    sections = lax.axis_size("slab")
    owners = lax.axis_size("pos")
    assert blocks >= 2 and sections & (sections - 1) == 0
    section = lax.axis_index("slab").reshape(1)
    sizes = dict(slots=slots, layers=layers, length=length, blocks=blocks)
    tile_shape = jax.ShapeDtypeStruct((layers, slots, 2, length, length), jnp.bfloat16)
    window = pltpu.VMEM((slots, 2, layers, length, 2 * length), jnp.float32)

    def ring(block, distance):
        route = [(i, (i + distance) % owners) for i in range(owners)]
        return lax.ppermute(block, "pos", route)

    def swap(block, bit):
        return lax.ppermute(block, "slab", [(i, i ^ bit) for i in range(sections)])

    own = jnp.concatenate([scan_coords.reshape(-1), scan_counts])
    theirs = ring(own, 1)
    tiles = pl.pallas_call(
        functools.partial(cut_kernel, **sizes),
        out_shape=tile_shape,
        in_specs=[spec(SMEM), spec(ANY)],
        out_specs=spec(VMEM),
        scratch_shapes=[window, pltpu.SemaphoreType.DMA((slots,))],
        name="cut",
    )(own, object_field)
    received = ring(tiles, 1)
    samples = ring(measured.astype(jnp.bfloat16), 1)
    merged = pl.pallas_call(
        functools.partial(merge_kernel, **sizes),
        out_shape=tile_shape,
        in_specs=[spec(SMEM), spec(ANY), spec(VMEM)],
        out_specs=spec(VMEM),
        scratch_shapes=[window, pltpu.SemaphoreType.DMA((slots,))],
        name="merge",
    )(theirs, object_field, received)
    gathered = {0: merged}
    bit = sections // 2
    while bit:
        for offset in list(gathered):
            gathered[offset | bit] = swap(gathered[offset], bit)
        bit //= 2
    field_shape = pltpu.VMEM((sections * layers, slots, 2, length, length), jnp.float32)
    grads = pl.pallas_call(
        functools.partial(chain_kernel, sections=sections, **sizes),
        out_shape=tile_shape,
        in_specs=[spec(SMEM), spec(SMEM)] + [spec(VMEM)] * (sections + 3),
        out_specs=spec(VMEM),
        scratch_shapes=[
            pltpu.VMEM((sections * layers, slots, 2, length, length), jnp.bfloat16),
            field_shape,
            field_shape,
        ],
        name="chain",
    )(
        theirs,
        section,
        *[gathered[offset] for offset in range(sections)],
        probe_wave,
        samples,
        jnp.asarray(chain_tables(length)),
    )
    returned = ring(grads, -1)
    return pl.pallas_call(
        functools.partial(add_kernel, **sizes),
        out_shape=jax.ShapeDtypeStruct(object_field.shape, jnp.float32),
        in_specs=[spec(SMEM), spec(SMEM), spec(VMEM), spec(VMEM)],
        out_specs=spec(ANY),
        scratch_shapes=[
            pltpu.VMEM(object_field.shape, jnp.float32),
            pltpu.SemaphoreType.DMA,
        ],
        name="add",
    )(own, theirs, grads, returned)


def solution(mesh):
    in_specs = (P(None, "slab", "pos", None), P(), P("pos", None), P("pos"), P("pos", None, None))
    out_specs = P(None, "slab", "pos", None)
    return jax.shard_map(
        per_device, mesh=mesh, in_specs=in_specs, out_specs=out_specs, check_vma=False
    )
```
